32 devices in a mesh: parts: 2 (over y), tile: 4 (over x, core), chan: 4 (over z).
Axes of the slice: x: 2, y: 2, z: 4, core: 2. Of those that a mesh axis runs over, the one named last changes fastest.
Arguments:
- weather: bfloat16 [768, 64, 1440], P('chan', 'parts', 'tile'), parts along dimension 1, may hold values from -6 to 6
- lon_taps: float32 [9, 768], P(None, 'chan'), may hold values from -4 to 4
- latitude_taps: float32 [9, 768], P(None, 'chan'), may hold values from -2 to 2
- norm_gain: float32 [768], replicated, may hold values from 0.1 to 1.9
- up_weight: bfloat16 [768, 3072], P(None, ('tile', 'chan')), may hold values from -0.21875 to 0.21875
- down_weight: bfloat16 [768, 3072], P(None, ('tile', 'chan')), may hold values from -0.109375 to 0.109375
Outputs:
- mixed: bfloat16 [768, 64, 1440], P('chan', 'parts', 'tile'), parts along dimension 1
The draws below stay inside these ranges and needn't reach their ends.
There are 2 independent parts, one for each index of `parts`. The reference program is written for one: setup_inputs(seed, part) draws one part's arguments, and reference() takes and returns one part's arrays. A program takes and returns all parts, laid end to end along the dimension named above; an argument that names none is the same for every part. Nothing has to cross between parts.
All inputs are finite; a program needn't handle non-finite values.
Results may differ from the reference program's by a relative error of at most 0.0065.
Values may be sent and summed in bfloat16 or wider, within the bound.
No kernel may reach another device: no remote copies, remote signals or barrier semaphores. Data moves between devices by JAX's collectives and lax.ppermute only.
A program may use at most 128 MiB of HBM per device.

```python
import math
import jax
import jax.numpy as jnp
from jax import lax

D = 768
FF = 3072
KERNEL_TAPS = 9
DILATION_STEP = 2
LATITUDE_ROWS = 32
LON = 1440
N_TILE = 4
N_CHAN = 4


def draw_lon_taps(key, part):
    scale_key, base_key = jax.random.split(key)
    channel_scale = 0.1 * jnp.exp(jax.random.uniform(scale_key, (1, D), jnp.float32, 0.0, math.log(10.0)))
    base_taps = jnp.clip(jax.random.normal(base_key, (KERNEL_TAPS, D), jnp.float32), -4.0, 4.0)
    return (base_taps * channel_scale).astype(jnp.float32)


def levels(stream_key, dims, pieces, least, high):
    def one(dim, parts):
        heights = jax.random.uniform(jax.random.fold_in(jax.random.fold_in(stream_key, 6), dim), (parts,), jnp.float32, least / len(pieces), high / len(pieces))
        return jnp.repeat(jnp.exp(heights), dims[dim] // parts).reshape((-1,) + (1,) * (len(dims) - dim - 1))

    loudness = one(*pieces[0])
    for cut in pieces[1:]:
        loudness = loudness * one(*cut)
    return loudness


def bell_draw(key, shape, scale, reach, cuts=(), held_as=jnp.bfloat16):
    result = scale * jax.random.normal(key, shape, jnp.float32)
    if cuts:
        result = result * levels(key, shape, cuts, -0.22, 0.18)
    return jnp.clip(result, -reach, reach).astype(held_as)


def setup_inputs(seed: int = 0, part: int = 0) -> dict:
    seeds = jax.random.split(jax.random.key(seed), 7)
    part_keys = jax.random.split(jax.random.fold_in(seeds[6], part), 7)
    return {
        "weather": bell_draw(part_keys[0], (D, LATITUDE_ROWS, LON), 1.0, 6.0, ((0, 4), (2, 4))),
        "lon_taps": draw_lon_taps(jax.random.fold_in(seeds[6], 71), part),
        "latitude_taps": bell_draw(seeds[2], (KERNEL_TAPS, D), 0.33, 2.0, ((1, 4),), jnp.float32),
        "norm_gain": jnp.clip(1.0 + 0.18 * jax.random.normal(seeds[3], (D,), jnp.float32), 0.1, 1.9),
        "up_weight": bell_draw(seeds[4], (D, FF), D ** -0.5, 0.21875, ((1, 16),)),
        "down_weight": bell_draw(seeds[5], (D, FF), FF ** -0.5, 0.109375, ((1, 16),)),
    }


def layer_norm(values, norm_gain):
    as_float = values.astype(jnp.float32)
    center = lax.optimization_barrier(jnp.mean(as_float, axis=0))
    deviation = as_float - center
    spread_sq = lax.optimization_barrier(jnp.mean(deviation * deviation, axis=0))
    return (deviation * lax.rsqrt(spread_sq + 1e-06) * norm_gain[:, None]).astype(jnp.bfloat16)

def grouped_update(down_weight, hidden):
    shard_width = FF // (N_TILE * N_CHAN)
    cell_count = hidden.shape[1]
    down_groups = down_weight.reshape(D, N_TILE, N_CHAN, shard_width)
    hidden_groups = hidden.reshape(N_TILE, N_CHAN, shard_width, cell_count)
    total = jnp.zeros((D, cell_count), jnp.float32)
    for group in range(N_CHAN):
        weights = down_groups[:, :, group, :].reshape(D, N_TILE * shard_width)
        rows = hidden_groups[:, group].reshape(N_TILE * shard_width, cell_count)
        partial_value = jnp.dot(weights, rows, preferred_element_type=jnp.float32).astype(jnp.bfloat16)
        partial_value = lax.optimization_barrier(partial_value)
        total = total + partial_value.astype(jnp.float32)
    return total.astype(jnp.bfloat16)

def reference(weather, lon_taps, latitude_taps, norm_gain, up_weight, down_weight):
    as_float = weather.astype(jnp.float32)
    lon_sum = jnp.zeros(weather.shape, jnp.float32)
    for kernel_tap_index in range(KERNEL_TAPS):
        shift_amount = DILATION_STEP * (kernel_tap_index - KERNEL_TAPS // 2)
        lon_sum = lon_sum + lon_taps[kernel_tap_index][:, None, None] * jnp.roll(as_float, -shift_amount, axis=2)
    border_width = DILATION_STEP * (KERNEL_TAPS // 2)
    padded_field = jnp.pad(lon_sum, ((0, 0), (border_width, border_width), (0, 0)))
    latitude_sum = jnp.zeros(weather.shape, jnp.float32)
    for kernel_tap_index in range(KERNEL_TAPS):
        latitude_sum = latitude_sum + latitude_taps[kernel_tap_index][:, None, None] * padded_field[:, DILATION_STEP * kernel_tap_index:DILATION_STEP * kernel_tap_index + LATITUDE_ROWS, :]
    spatial = latitude_sum.astype(jnp.bfloat16)

    def one_row(pair):
        spatial_row, input_row = pair
        normed = layer_norm(spatial_row, norm_gain)
        expanded = jnp.dot(up_weight.T, normed, preferred_element_type=jnp.float32)
        hidden = jax.nn.gelu(expanded, approximate=False).astype(jnp.bfloat16)
        update = grouped_update(down_weight, hidden)
        return (input_row.astype(jnp.float32) + update.astype(jnp.float32)).astype(jnp.bfloat16)
    mixed_rows = lax.map(one_row, (jnp.transpose(spatial, (1, 0, 2)), jnp.transpose(weather, (1, 0, 2))))
    return jnp.transpose(mixed_rows, (1, 0, 2))
```

```python
import functools

import jax
import jax.numpy as jnp
from jax import lax
from jax.experimental import pallas as pl
from jax.experimental.pallas import tpu as pltpu
from jax.sharding import PartitionSpec as P

KERNEL_TAPS = 9
DILATION_STEP = 2
BORDER = DILATION_STEP * (KERNEL_TAPS // 2)
LANES = 128
CHUNKS = 4
VMEM_BYTES = 60 * 1024 * 1024


def round_up(value, step):
    return -(-value // step) * step


def conv_kernel(first_row, row_count, field_ref, before_ref, after_ref, lon_ref, lat_ref, out_ref, base_ref):
    row_total, _, width = field_ref.shape
    wide = base_ref.shape[2]
    low = max(0, first_row - BORDER)
    high = min(row_total, first_row + row_count + BORDER)
    for row in range(low, high):
        base_ref[row - low, :, 0:width] = field_ref[row].astype(jnp.float32)
        base_ref[row - low, :, width : width + BORDER] = after_ref[row].astype(jnp.float32)
        base_ref[row - low, :, wide - BORDER : wide] = before_ref[row].astype(jnp.float32)
    block = base_ref.shape[1]
    lon = [jnp.broadcast_to(lon_ref[:, t : t + 1], (block, wide)) for t in range(KERNEL_TAPS)]
    lat = [jnp.broadcast_to(lat_ref[:, t : t + 1], (block, wide)) for t in range(KERNEL_TAPS)]
    for out_row in range(row_count):
        total = None
        for t in range(KERNEL_TAPS):
            row = first_row + out_row + DILATION_STEP * (t - KERNEL_TAPS // 2)
            if low <= row < high:
                term = lat[t] * base_ref[row - low]
                total = term if total is None else total + term
        result = lon[KERNEL_TAPS // 2] * total
        for t in range(KERNEL_TAPS):
            shift = DILATION_STEP * (t - KERNEL_TAPS // 2)
            if shift:
                result = result + lon[t] * pltpu.roll(total, (-shift) % wide, 1)
        out_ref[out_row] = result[:, 0:width].astype(out_ref.dtype)


def convolve(field, before, after, lon_taps, lat_taps, first_row, row_count):
    row_total, chan_count, width = field.shape
    block = 32
    wide = round_up(width + 2 * BORDER, LANES)
    held_rows = min(row_total, first_row + row_count + BORDER) - max(0, first_row - BORDER)
    return pl.pallas_call(
        functools.partial(conv_kernel, first_row, row_count),
        grid=(chan_count // block,),
        in_specs=[
            pl.BlockSpec((row_total, block, width), lambda c: (0, c, 0)),
            pl.BlockSpec((row_total, block, BORDER), lambda c: (0, c, 0)),
            pl.BlockSpec((row_total, block, BORDER), lambda c: (0, c, 0)),
            pl.BlockSpec((block, KERNEL_TAPS), lambda c: (c, 0)),
            pl.BlockSpec((block, KERNEL_TAPS), lambda c: (c, 0)),
        ],
        out_specs=pl.BlockSpec((row_count, block, width), lambda c: (0, c, 0)),
        out_shape=jax.ShapeDtypeStruct((row_count, chan_count, width), jnp.bfloat16),
        scratch_shapes=[pltpu.VMEM((held_rows, block, wide), jnp.float32)],
        compiler_params=pltpu.CompilerParams(vmem_limit_bytes=VMEM_BYTES),
        name="conv",
    )(field, before, after, lon_taps, lat_taps)


def mlp_kernel(sources, x_ref, gain_ref, up_ref, down_ref, out_ref, values, normed, total):
    step = pl.program_id(0)
    rows = x_ref.shape[0] // sources
    chan_count, width = x_ref.shape[1:]
    wide = values.shape[1] // rows

    @pl.when(step == 0)
    def _():
        for source in range(sources):
            for row in range(rows):
                values[source * chan_count : (source + 1) * chan_count, row * wide : row * wide + width] = x_ref[
                    source * rows + row
                ].astype(jnp.float32)
        as_float = values[...]
        center = jnp.mean(as_float, axis=0, keepdims=True)
        deviation = as_float - center
        spread_sq = jnp.mean(deviation * deviation, axis=0, keepdims=True)
        normed[...] = (deviation * lax.rsqrt(spread_sq + 1e-06) * gain_ref[...]).astype(jnp.bfloat16)
        total[...] = jnp.zeros_like(total)

    expanded = jnp.dot(up_ref[...], normed[...], preferred_element_type=jnp.float32)
    hidden = (0.5 * expanded * (1.0 + lax.erf(expanded * 0.7071067811865476))).astype(jnp.bfloat16)
    total[...] += jnp.dot(down_ref[...], hidden, preferred_element_type=jnp.float32)

    @pl.when(step == pl.num_programs(0) - 1)
    def _():
        for source in range(sources):
            for row in range(rows):
                out_ref[source * rows + row] = total[
                    source * chan_count : (source + 1) * chan_count, row * wide : row * wide + width
                ].astype(out_ref.dtype)


def mlp(x, sources, gain, up_all, down_all):
    row_count, chan_count, width = x.shape
    width_all, hidden_total = down_all.shape
    block = 512
    lanes = (row_count // sources) * round_up(width, LANES)
    return pl.pallas_call(
        functools.partial(mlp_kernel, sources),
        grid=(hidden_total // block,),
        in_specs=[
            pl.BlockSpec((row_count, chan_count, width), lambda h: (0, 0, 0)),
            pl.BlockSpec((width_all, 1), lambda h: (0, 0)),
            pl.BlockSpec((block, width_all), lambda h: (h, 0)),
            pl.BlockSpec((width_all, block), lambda h: (0, h)),
        ],
        out_specs=pl.BlockSpec((row_count, chan_count, width), lambda h: (0, 0, 0)),
        out_shape=jax.ShapeDtypeStruct(x.shape, jnp.bfloat16),
        scratch_shapes=[
            pltpu.VMEM((width_all, lanes), jnp.float32),
            pltpu.VMEM((width_all, lanes), jnp.bfloat16),
            pltpu.VMEM((width_all, lanes), jnp.float32),
        ],
        compiler_params=pltpu.CompilerParams(vmem_limit_bytes=VMEM_BYTES),
        name="mlp",
    )(x, gain, up_all, down_all)


def add_kernel(update_ref, field_ref, *rest):
    out_ref = rest[-1]
    update = jnp.transpose(update_ref[...].astype(jnp.float32), (1, 0, 2))
    out_ref[...] = (field_ref[...].astype(jnp.float32) + update).astype(out_ref.dtype)


def add_rows(update, field, done, place):
    row_count, chan_count, width = update.shape
    block = 32
    rows_of = pl.BlockSpec((block, row_count, width), lambda c: (c, place, 0))
    specs = [pl.BlockSpec((row_count, block, width), lambda c: (0, c, 0)), rows_of]
    operands = [update, field]
    if done is not None:
        specs.append(pl.BlockSpec(memory_space=pl.ANY))
        operands.append(done)
    return pl.pallas_call(
        add_kernel,
        grid=(chan_count // block,),
        in_specs=specs,
        out_specs=rows_of,
        out_shape=jax.ShapeDtypeStruct(field.shape, jnp.bfloat16),
        input_output_aliases={2: 0} if done is not None else {},
        compiler_params=pltpu.CompilerParams(vmem_limit_bytes=VMEM_BYTES),
        name="add",
    )(*operands)


def gather_weights(shard):
    chans = lax.axis_size("chan")
    held = [shard[None]]
    for shift in range(1, chans):
        held.append(lax.ppermute(shard[None], "chan", [(i, (i + shift) % chans) for i in range(chans)]))
    held = jnp.concatenate(held, axis=0)
    tiles = lax.axis_size("tile")
    bit = tiles // 2
    while bit:
        held = jnp.concatenate([held, lax.ppermute(held, "tile", [(i, i ^ bit) for i in range(tiles)])], axis=0)
        bit //= 2
    return held


def on_device(weather, lon_taps, latitude_taps, norm_gain, up_weight, down_weight):
    chan_count, row_total, width = weather.shape
    sources = lax.axis_size("chan")
    tiles = lax.axis_size("tile")
    up = [(i, (i + 1) % tiles) for i in range(tiles)]
    down = [(j, i) for i, j in up]
    before = lax.ppermute(weather[:, :, width - BORDER :], "tile", up)
    after = lax.ppermute(weather[:, :, :BORDER], "tile", down)
    shard_width = up_weight.shape[1]
    weights = gather_weights(jnp.concatenate([up_weight.T, down_weight.T], axis=0))
    up_all = weights[:, :shard_width].reshape(-1, up_weight.shape[0])
    down_all = weights[:, shard_width:].reshape(-1, up_weight.shape[0]).T
    field = jnp.transpose(weather, (1, 0, 2))
    before = jnp.transpose(before, (1, 0, 2))
    after = jnp.transpose(after, (1, 0, 2))
    lon, lat = lon_taps.T, latitude_taps.T
    rows = row_total // CHUNKS
    by_cell = []
    for chunk in range(CHUNKS):
        spatial = convolve(field, before, after, lon, lat, chunk * rows, rows)
        by_cell.append(lax.all_to_all(spatial, "chan", split_axis=0, concat_axis=0, tiled=True))
    gain = norm_gain[:, None]
    updates = []
    for chunk in range(CHUNKS):
        update = mlp(by_cell[chunk], sources, gain, up_all, down_all)
        updates.append(lax.all_to_all(update, "chan", split_axis=0, concat_axis=0, tiled=True))
    mixed = None
    for chunk in range(CHUNKS):
        mixed = add_rows(updates[chunk], weather, mixed, chunk)
    return mixed


def solution(mesh):
    return jax.shard_map(
        on_device,
        mesh=mesh,
        in_specs=(
            P("chan", "parts", "tile"),
            P(None, "chan"),
            P(None, "chan"),
            P(),
            P(None, ("tile", "chan")),
            P(None, ("tile", "chan")),
        ),
        out_specs=P("chan", "parts", "tile"),
        check_vma=False,
    )
```

```python
import functools

import jax
import jax.numpy as jnp
from jax import lax
from jax.experimental import pallas as pl
from jax.experimental.pallas import tpu as pltpu
from jax.sharding import PartitionSpec as P

KERNEL_TAPS = 9
DILATION_STEP = 2
BORDER = DILATION_STEP * (KERNEL_TAPS // 2)
LANES = 128
SUBLANES = 8
CHUNKS = 4
PARAMS = pltpu.CompilerParams(vmem_limit_bytes=60 * 1024 * 1024)


def microseconds(count):
    return pl.CostEstimate(flops=int(count * 1.15e8), bytes_accessed=1024, transcendentals=0)


def round_up(value, step):
    return -(-value // step) * step


class Packing:
    def __init__(self, chan_count, cells):
        self.block = 64 if chan_count % 64 == 0 else 32
        self.blocks = chan_count // self.block
        unit = LANES * SUBLANES // self.block
        used = round_up(cells, unit)
        self.full = used // LANES
        self.groups = []
        row, offset, size = self.full * self.block, 0, LANES // 2
        while size >= unit:
            if used % LANES & size:
                self.groups.append((row, offset, size))
                row += self.block * size // LANES
                offset += size
            size //= 2
        self.rows = row
        self.wide = round_up(cells, LANES)

    def store(self, ref, lead, load):
        for i in range(self.full):
            ref[lead, i * self.block : (i + 1) * self.block, :] = load(i).astype(ref.dtype)
        if not self.groups:
            return
        tail = load(self.full)
        for row, offset, size in self.groups:
            count = self.block * size // LANES
            lane = lax.broadcasted_iota(jnp.int32, (count, LANES), 1)
            packed = None
            for g in range(LANES // size):
                piece = tail[g * count : (g + 1) * count]
                if (g * size - offset) % LANES:
                    piece = pltpu.roll(piece, (g * size - offset) % LANES, 1)
                packed = piece if packed is None else jnp.where(lane >= g * size, piece, packed)
            ref[lead, row : row + count, :] = packed.astype(ref.dtype)

    def load(self, ref, lead, store):
        for i in range(self.full):
            store(i, ref[lead, i * self.block : (i + 1) * self.block, :].astype(jnp.float32))
        if not self.groups:
            return
        lane = lax.broadcasted_iota(jnp.int32, (self.block, LANES), 1)
        tail = None
        for row, offset, size in self.groups:
            count = self.block * size // LANES
            packed = ref[lead, row : row + count, :].astype(jnp.float32)
            pieces = []
            for g in range(LANES // size):
                turn = (offset - g * size) % LANES
                pieces.append(pltpu.roll(packed, turn, 1) if turn else packed)
            whole = jnp.concatenate(pieces, axis=0)
            tail = whole if tail is None else jnp.where(lane >= offset, whole, tail)
        store(self.full, tail)


def conv_kernel(packing, sources, rows, first_row, low, me_ref, *refs):
    field_refs, (lon_ref, lat_ref), out_refs = refs[: -sources - 4], refs[-sources - 4 : -sources - 2], refs[-sources - 2 : -2]
    base_ref, cells_ref = refs[-2:]
    width = field_refs[0].shape[2]
    held_rows, block, wide = base_ref.shape
    group = field_refs[0].shape[0]
    for held in range(held_rows):
        field_ref, before_ref, after_ref = field_refs[held // group * 3 : held // group * 3 + 3]
        row = held % group
        base_ref[held, :, 0:width] = field_ref[row].astype(jnp.float32)
        base_ref[held, :, width : width + BORDER] = after_ref[row].astype(jnp.float32)
        base_ref[held, :, wide - BORDER : wide] = before_ref[row].astype(jnp.float32)
    me = me_ref[0]
    part = 16

    def some_channels(index, _):
        chans = pl.ds(pl.multiple_of(index * part, part), part)
        lon = [jnp.broadcast_to(lon_ref[chans, t : t + 1], (part, wide)) for t in range(KERNEL_TAPS)]
        lat = [jnp.broadcast_to(lat_ref[chans, t : t + 1], (part, wide)) for t in range(KERNEL_TAPS)]
        for out_row in range(sources * rows):
            total = None
            for t in range(KERNEL_TAPS):
                held = first_row + out_row + DILATION_STEP * (t - KERNEL_TAPS // 2) - low
                if 0 <= held < held_rows:
                    term = lat[t] * base_ref[held, chans, :]
                    total = term if total is None else total + term
            result = lon[KERNEL_TAPS // 2] * total
            for t in range(KERNEL_TAPS):
                turn = DILATION_STEP * (KERNEL_TAPS // 2 - t)
                if turn:
                    result = result + lon[t] * pltpu.roll(total, turn % wide, 1)
            receiver, row = divmod(out_row, rows)
            shift = lax.rem(receiver + sources - me, sources)
            cells_ref[shift, chans, row * width : (row + 1) * width] = result[:, 0:width]
        return 0

    lax.fori_loop(0, block // part, some_channels, 0)
    for shift in range(sources):
        packing.store(out_refs[shift], 0, lambda i: cells_ref[shift, :, i * LANES : (i + 1) * LANES])


def convolve(packing, me, sources, field, before, after, lon_taps, lat_taps, place, row_count):
    row_total, chan_count, width = field.shape
    block = packing.block
    wide = round_up(width + 2 * BORDER, LANES)
    piece = jax.ShapeDtypeStruct((packing.blocks, packing.rows, LANES), jnp.bfloat16)
    reach = -(-BORDER // row_count)
    places = range(max(0, place - reach), min(row_total // row_count, place + reach + 1))
    specs, operands = [], []
    for near in places:
        for array in (field, before, after):
            specs.append(pl.BlockSpec((row_count, block, array.shape[2]), lambda c, me, near=near: (near, c, 0)))
            operands.append(array)
    taps = pl.BlockSpec((block, KERNEL_TAPS), lambda c, me: (c, 0))
    return pl.pallas_call(
        functools.partial(
            conv_kernel, packing, sources, row_count // sources, place * row_count, places[0] * row_count
        ),
        grid_spec=pltpu.PrefetchScalarGridSpec(
            num_scalar_prefetch=1,
            grid=(packing.blocks,),
            in_specs=[*specs, taps, taps],
            out_specs=[pl.BlockSpec((1, packing.rows, LANES), lambda c, me: (c, 0, 0))] * sources,
            scratch_shapes=[
                pltpu.VMEM((len(places) * row_count, block, wide), jnp.float32),
                pltpu.VMEM((sources, block, packing.wide), jnp.float32),
            ],
        ),
        out_shape=[piece] * sources,
        compiler_params=PARAMS,
        cost_estimate=microseconds(12),
        name="conv",
    )(me, *operands, lon_taps, lat_taps)


def mlp_kernel(packing, sources, me_ref, *refs):
    x_refs, (gain_ref, up_ref, down_ref) = refs[:sources], refs[sources : sources + 3]
    out_refs, (values, normed, total) = refs[sources + 3 : -3], refs[-3:]
    step = pl.program_id(0)
    me = me_ref[0]
    block = packing.block
    chan_count = packing.blocks * block

    def channels(owner, lead):
        return pl.ds(pl.multiple_of(owner * chan_count + lead * block, SUBLANES), block)

    @pl.when(step == 0)
    def _():
        for shift in range(sources):
            sender = lax.rem(me + sources - shift, sources)
            for lead in range(packing.blocks):

                def put(i, piece, at=channels(sender, lead)):
                    values[at, i * LANES : (i + 1) * LANES] = piece

                packing.load(x_refs[shift], lead, put)
        as_float = values[...]
        center = jnp.mean(as_float, axis=0, keepdims=True)
        deviation = as_float - center
        spread_sq = jnp.mean(deviation * deviation, axis=0, keepdims=True)
        normed[...] = (deviation * lax.rsqrt(spread_sq + 1e-06) * gain_ref[...]).astype(jnp.bfloat16)
        total[...] = jnp.zeros_like(total)

    expanded = jnp.dot(up_ref[...], normed[...], preferred_element_type=jnp.float32)
    hidden = (0.5 * expanded * (1.0 + lax.erf(expanded * 0.7071067811865476))).astype(jnp.bfloat16)
    total[...] += jnp.dot(down_ref[...], hidden, preferred_element_type=jnp.float32)

    @pl.when(step == pl.num_programs(0) - 1)
    def _():
        for shift in range(sources):
            owner = lax.rem(me + shift, sources)
            for lead in range(packing.blocks):
                at = channels(owner, lead)
                packing.store(out_refs[shift], lead, lambda i: total[at, i * LANES : (i + 1) * LANES])


def mlp(packing, me, pieces, gain, up_all, down_all):
    sources = len(pieces)
    width_all, hidden_total = down_all.shape
    block = 512
    whole = pl.BlockSpec(pieces[0].shape, lambda h, me: (0, 0, 0))
    return pl.pallas_call(
        functools.partial(mlp_kernel, packing, sources),
        grid_spec=pltpu.PrefetchScalarGridSpec(
            num_scalar_prefetch=1,
            grid=(hidden_total // block,),
            in_specs=[whole] * sources
            + [
                pl.BlockSpec((width_all, 1), lambda h, me: (0, 0)),
                pl.BlockSpec((block, width_all), lambda h, me: (h, 0)),
                pl.BlockSpec((width_all, block), lambda h, me: (0, h)),
            ],
            out_specs=[whole] * sources,
            scratch_shapes=[
                pltpu.VMEM((width_all, packing.wide), jnp.float32),
                pltpu.VMEM((width_all, packing.wide), jnp.bfloat16),
                pltpu.VMEM((width_all, packing.wide), jnp.float32),
            ],
        ),
        out_shape=[jax.ShapeDtypeStruct(pieces[0].shape, jnp.bfloat16)] * sources,
        compiler_params=PARAMS,
        cost_estimate=microseconds(13),
        name="mlp",
    )(me, *pieces, gain, up_all, down_all)


def add_kernel(packing, sources, me_ref, *refs):
    piece_refs, field_ref = refs[:sources], refs[sources]
    out_ref, cells_ref, update_ref = refs[-3:]
    me = me_ref[0]
    rows = update_ref.shape[0] // sources
    width = field_ref.shape[2]
    for shift in range(sources):
        sender = lax.rem(me + sources - shift, sources)

        def put(i, piece):
            cells_ref[:, i * LANES : (i + 1) * LANES] = piece

        packing.load(piece_refs[shift], 0, put)
        for row in range(rows):
            update_ref[sender * rows + row] = cells_ref[:, row * width : (row + 1) * width]
    update = jnp.transpose(update_ref[...], (1, 0, 2))
    out_ref[...] = (field_ref[...].astype(jnp.float32) + update).astype(out_ref.dtype)


def add_rows(packing, me, pieces, field, done, place, row_count):
    sources = len(pieces)
    width = field.shape[2]
    block = packing.block
    rows_of = pl.BlockSpec((block, row_count, width), lambda c, me: (c, place, 0))
    specs = [pl.BlockSpec((1, packing.rows, LANES), lambda c, me: (c, 0, 0))] * sources + [rows_of]
    operands = [me, *pieces, field]
    if done is not None:
        specs.append(pl.BlockSpec(memory_space=pl.ANY))
        operands.append(done)
    return pl.pallas_call(
        functools.partial(add_kernel, packing, sources),
        grid_spec=pltpu.PrefetchScalarGridSpec(
            num_scalar_prefetch=1,
            grid=(packing.blocks,),
            in_specs=specs,
            out_specs=rows_of,
            scratch_shapes=[
                pltpu.VMEM((block, packing.wide), jnp.float32),
                pltpu.VMEM((row_count, block, width), jnp.float32),
            ],
        ),
        out_shape=jax.ShapeDtypeStruct(field.shape, jnp.bfloat16),
        input_output_aliases={len(operands) - 1: 0} if done is not None else {},
        compiler_params=PARAMS,
        cost_estimate=microseconds(4),
        name="add",
    )(*operands)


def prepare_kernel(held_ref, received_ref, *refs):
    up_ref, down_ref = refs[-2:]
    half = held_ref.shape[1] // 2
    up_ref[0:half] = held_ref[0, 0:half]
    up_ref[half:] = received_ref[0, 0:half]
    down_ref[:, 0:half] = held_ref[0, half:].T
    down_ref[:, half:] = received_ref[0, half:].T


def prepare(held, received, total, done, place):
    count, rows, width = held.shape
    if rows % LANES:
        both = jnp.concatenate([held, received], axis=0)
        half = rows // 2
        return both[:, :half].reshape(total, width), both[:, half:].reshape(total, width).T
    source = pl.BlockSpec((1, rows, width), lambda i: (i, 0, 0))
    return pl.pallas_call(
        prepare_kernel,
        grid=(count,),
        in_specs=[source, source] + [pl.BlockSpec(memory_space=pl.ANY)] * len(done),
        out_specs=[
            pl.BlockSpec((rows, width), lambda i: (place + i, 0)),
            pl.BlockSpec((width, rows), lambda i: (0, place + i)),
        ],
        out_shape=[
            jax.ShapeDtypeStruct((total, width), held.dtype),
            jax.ShapeDtypeStruct((width, total), held.dtype),
        ],
        input_output_aliases={2: 0, 3: 1} if done else {},
        compiler_params=PARAMS,
        cost_estimate=microseconds(count),
        name="prepare",
    )(held, received, *done)


def shifted(array, axis, shift):
    count = lax.axis_size(axis)
    return lax.ppermute(array, axis, [(i, (i + shift) % count) for i in range(count)])


def exchanged(array, axis, bit):
    return lax.ppermute(array, axis, [(i, i ^ bit) for i in range(lax.axis_size(axis))])


def after_all(arrays, *others):
    return lax.optimization_barrier((arrays, others))[0]


def on_device(weather, lon_taps, latitude_taps, norm_gain, up_weight, down_weight):
    chan_count, row_total, width = weather.shape
    sources, tiles = lax.axis_size("chan"), lax.axis_size("tile")
    me = lax.axis_index("chan").astype(jnp.int32)[None]
    with jax.named_scope("halo"):
        before = shifted(weather[:, :, width - BORDER :], "tile", 1)
        after = shifted(weather[:, :, :BORDER], "tile", tiles - 1)
    shard = jnp.concatenate([up_weight.T, down_weight.T], axis=0)[None]
    with jax.named_scope("wz"):
        far = [shard]
        bit = sources // 2
        while bit > 1:
            far = far + [exchanged(piece, "chan", bit) for piece in far]
            bit //= 2
        near = exchanged(shard, "chan", 1)
    bits = []
    bit = tiles // 2
    while bit > 1:
        bits.append(bit)
        bit //= 2
    with jax.named_scope("wx0"):
        across = exchanged(shard, "tile", bits[0])
    field = jnp.transpose(weather, (1, 0, 2))
    before = jnp.transpose(before, (1, 0, 2))
    after = jnp.transpose(after, (1, 0, 2))
    lon, lat = lon_taps.T, latitude_taps.T
    rows = row_total // CHUNKS
    hidden_total = sources * tiles * up_weight.shape[1]
    packing = Packing(chan_count, rows // sources * width)

    def spread(chunk):
        pieces = convolve(packing, me, sources, field, before, after, lon, lat, chunk, rows)
        with jax.named_scope(f"in{chunk}"):
            return [pieces[0]] + [shifted(pieces[s], "chan", s) for s in range(1, sources)]

    by_cell = [spread(0)]
    lon, far, near, across = after_all((lon, far, near, across), by_cell[0][0])
    with jax.named_scope("wz1"):
        rest = [exchanged(piece, "chan", 1) for piece in far[1:]]
    by_cell.append(spread(1))
    lon, rest = after_all((lon, rest), by_cell[1][0], by_cell[0][1:])
    others = jnp.concatenate([*far[1:], near, *rest], axis=0)
    with jax.named_scope("wx1"):
        others_across = exchanged(others, "tile", bits[0])
    by_cell.append(spread(2))
    lon, others, across = after_all((lon, others, across), by_cell[2][0], by_cell[1][1:])
    if len(bits) == 1:
        held = jnp.concatenate([shard, others, across], axis=0)
        with jax.named_scope("wc0"):
            received = exchanged(held, "tile", 1)
    by_cell.append(spread(3))
    others_across = after_all(others_across, by_cell[3][:2], by_cell[2][1:])
    weights, place = (), 0
    if len(bits) == 1:
        weights, place = prepare(held, received, hidden_total, (), 0), held.shape[0]
        held = others_across
    else:
        held = jnp.concatenate([shard, others, across, others_across], axis=0)
        for bit in bits[1:]:
            held = jnp.concatenate([held, exchanged(held, "tile", bit)], axis=0)
    with jax.named_scope("wc1"):
        received = exchanged(held, "tile", 1)
    up_all, down_all = prepare(held, received, hidden_total, weights, place)
    gain = norm_gain[:, None]
    updates = []
    for chunk in range(CHUNKS):
        pieces = mlp(packing, me, by_cell[chunk], gain, up_all, down_all)
        with jax.named_scope(f"out{chunk}"):
            updates.append([pieces[0]] + [shifted(pieces[s], "chan", s) for s in range(1, sources)])
        gain = after_all(gain, pieces[0], updates[chunk - 1][1:] if chunk else by_cell[CHUNKS - 1][1:])
    mixed = None
    for chunk in range(CHUNKS):
        mixed = add_rows(packing, me, updates[chunk], weather, mixed, chunk, rows)
    return mixed


def solution(mesh):
    return jax.shard_map(
        on_device,
        mesh=mesh,
        in_specs=(
            P("chan", "parts", "tile"),
            P(None, "chan"),
            P(None, "chan"),
            P(),
            P(None, ("tile", "chan")),
            P(None, ("tile", "chan")),
        ),
        out_specs=P("chan", "parts", "tile"),
        check_vma=False,
    )
```

```python
import functools

import jax
import jax.numpy as jnp
from jax import lax
from jax.experimental import pallas as pl
from jax.experimental.pallas import tpu as pltpu
from jax.sharding import PartitionSpec as P

KERNEL_TAPS = 9
DILATION_STEP = 2
BORDER = DILATION_STEP * (KERNEL_TAPS // 2)
LANES = 128
SUBLANES = 8
CHUNKS = 4
PARAMS = pltpu.CompilerParams(vmem_limit_bytes=60 * 1024 * 1024)


def microseconds(count):
    return pl.CostEstimate(flops=int(count * 1.15e9), bytes_accessed=1024, transcendentals=0)


def round_up(value, step):
    return -(-value // step) * step


class Packing:
    def __init__(self, chan_count, cells):
        self.block = 64 if chan_count % 64 == 0 else 32
        self.blocks = chan_count // self.block
        unit = LANES * SUBLANES // self.block
        used = round_up(cells, unit)
        self.full = used // LANES
        self.groups = []
        row, offset, size = self.full * self.block, 0, LANES // 2
        while size >= unit:
            if used % LANES & size:
                self.groups.append((row, offset, size))
                row += self.block * size // LANES
                offset += size
            size //= 2
        self.rows = row
        self.wide = round_up(cells, LANES)

    def store(self, ref, lead, load):
        for i in range(self.full):
            ref[lead, i * self.block : (i + 1) * self.block, :] = load(i).astype(ref.dtype)
        if not self.groups:
            return
        tail = load(self.full)
        for row, offset, size in self.groups:
            count = self.block * size // LANES
            lane = lax.broadcasted_iota(jnp.int32, (count, LANES), 1)
            packed = None
            for g in range(LANES // size):
                piece = tail[g * count : (g + 1) * count]
                if (g * size - offset) % LANES:
                    piece = pltpu.roll(piece, (g * size - offset) % LANES, 1)
                packed = piece if packed is None else jnp.where(lane >= g * size, piece, packed)
            ref[lead, row : row + count, :] = packed.astype(ref.dtype)

    def load(self, ref, lead, store):
        for i in range(self.full):
            store(i, ref[lead, i * self.block : (i + 1) * self.block, :].astype(jnp.float32))
        if not self.groups:
            return
        lane = lax.broadcasted_iota(jnp.int32, (self.block, LANES), 1)
        tail = None
        for row, offset, size in self.groups:
            count = self.block * size // LANES
            packed = ref[lead, row : row + count, :].astype(jnp.float32)
            pieces = []
            for g in range(LANES // size):
                turn = (offset - g * size) % LANES
                pieces.append(pltpu.roll(packed, turn, 1) if turn else packed)
            whole = jnp.concatenate(pieces, axis=0)
            tail = whole if tail is None else jnp.where(lane >= offset, whole, tail)
        store(self.full, tail)


def conv_kernel(packing, sources, rows, first_row, low, *refs):
    *field_refs, lon_ref, lat_ref, out_ref, base_ref, cells_ref = refs
    width = field_refs[0].shape[2]
    held_rows, block, wide = base_ref.shape
    group = field_refs[0].shape[0]
    for held in range(held_rows):
        field_ref, before_ref, after_ref = field_refs[held // group * 3 : held // group * 3 + 3]
        row = held % group
        base_ref[held, :, 0:width] = field_ref[row].astype(jnp.float32)
        base_ref[held, :, width : width + BORDER] = after_ref[row].astype(jnp.float32)
        base_ref[held, :, wide - BORDER : wide] = before_ref[row].astype(jnp.float32)
    part = 16

    def some_channels(index, _):
        chans = pl.ds(pl.multiple_of(index * part, part), part)
        lon = [jnp.broadcast_to(lon_ref[chans, t : t + 1], (part, wide)) for t in range(KERNEL_TAPS)]
        lat = [jnp.broadcast_to(lat_ref[chans, t : t + 1], (part, wide)) for t in range(KERNEL_TAPS)]
        for out_row in range(sources * rows):
            total = None
            for t in range(KERNEL_TAPS):
                held = first_row + out_row + DILATION_STEP * (t - KERNEL_TAPS // 2) - low
                if 0 <= held < held_rows:
                    term = lat[t] * base_ref[held, chans, :]
                    total = term if total is None else total + term
            near = [total if turn == 0 else pltpu.roll(total, turn % wide, 1) for turn in (2, 0, -2)]
            result = None
            for a, turn in enumerate((6, 0, -6)):
                term = lon[3 * a] * near[0] + lon[3 * a + 1] * near[1] + lon[3 * a + 2] * near[2]
                term = pltpu.roll(term, turn % wide, 1) if turn else term
                result = term if result is None else result + term
            receiver, row = divmod(out_row, rows)
            cells_ref[receiver, chans, row * width : (row + 1) * width] = result[:, 0:width]
        return 0

    lax.fori_loop(0, block // part, some_channels, 0)
    for receiver in range(sources):
        packing.store(out_ref.at[receiver], 0, lambda i: cells_ref[receiver, :, i * LANES : (i + 1) * LANES])


def convolve(packing, sources, field, before, after, lon_taps, lat_taps, place, row_count):
    row_total, chan_count, width = field.shape
    block = packing.block
    wide = round_up(width + 2 * BORDER, LANES)
    reach = -(-BORDER // row_count)
    places = range(max(0, place - reach), min(row_total // row_count, place + 1 + reach))
    specs, operands = [], []
    for near in places:
        for array in (field, before, after):
            specs.append(pl.BlockSpec((row_count, block, array.shape[2]), lambda c, near=near: (near, c, 0)))
            operands.append(array)
    taps = pl.BlockSpec((block, KERNEL_TAPS), lambda c: (c, 0))
    return pl.pallas_call(
        functools.partial(
            conv_kernel, packing, sources, row_count // sources, place * row_count, places[0] * row_count
        ),
        grid=(packing.blocks,),
        in_specs=[*specs, taps, taps],
        out_specs=pl.BlockSpec((sources, 1, packing.rows, LANES), lambda c: (0, c, 0, 0)),
        out_shape=jax.ShapeDtypeStruct((sources, packing.blocks, packing.rows, LANES), jnp.bfloat16),
        scratch_shapes=[
            pltpu.VMEM((len(places) * row_count, block, wide), jnp.float32),
            pltpu.VMEM((sources, block, packing.wide), jnp.float32),
        ],
        compiler_params=PARAMS,
        cost_estimate=microseconds(12),
        name="conv",
    )(*operands, lon_taps, lat_taps)


def mlp_kernel(packing, sources, counts, me_ref, *refs):
    x_ref, gain_ref = refs[:2]
    weight_refs = refs[2 : 2 + 2 * len(counts)]
    out_refs, (values, normed, total) = refs[-sources - 3 : -3], refs[-3:]
    step = pl.program_id(0)
    me = me_ref[0]
    block = packing.block
    chan_count = packing.blocks * block

    def channels(owner, lead):
        start = owner * chan_count + lead * block
        return pl.ds(start if isinstance(start, int) else pl.multiple_of(start, SUBLANES), block)

    @pl.when(step == 0)
    def _():
        for sender in range(sources):
            for lead in range(packing.blocks):

                def put(i, piece, at=channels(sender, lead)):
                    values[at, i * LANES : (i + 1) * LANES] = piece

                packing.load(x_ref.at[sender], lead, put)
        as_float = values[...]
        center = jnp.mean(as_float, axis=0, keepdims=True)
        deviation = as_float - center
        spread_sq = jnp.mean(deviation * deviation, axis=0, keepdims=True)
        normed[...] = (deviation * lax.rsqrt(spread_sq + 1e-06) * gain_ref[...]).astype(jnp.bfloat16)
        total[...] = jnp.zeros_like(total)

    first = 0
    for index, count in enumerate(counts):

        @pl.when(jnp.logical_and(step >= first, step < first + count))
        def _(pair=weight_refs[2 * index : 2 * index + 2]):
            hidden, down = [], []
            for ref in pair:
                whole = ref[...]
                half = whole.shape[1] // 2
                up_rows = whole[:, :half].reshape(-1, whole.shape[2])
                expanded = jnp.dot(up_rows, normed[...], preferred_element_type=jnp.float32)
                gelu = 0.5 * expanded * (1.0 + lax.erf(expanded * 0.7071067811865476))
                hidden.append(gelu.astype(jnp.bfloat16))
                down.append(whole[:, half:].reshape(-1, whole.shape[2]))
            total[...] += lax.dot_general(
                jnp.concatenate(down, axis=0),
                jnp.concatenate(hidden, axis=0),
                (((0,), (0,)), ((), ())),
                preferred_element_type=jnp.float32,
            )

        first += count

    @pl.when(step == pl.num_programs(0) - 1)
    def _():
        for shift in range(sources):
            owner = lax.rem(me + shift, sources)
            for lead in range(packing.blocks):
                at = channels(owner, lead)
                packing.store(out_refs[shift], lead, lambda i: total[at, i * LANES : (i + 1) * LANES])


def mlp(packing, me, by_cell, gain, weights):
    sources = by_cell.shape[0]
    width_all = gain.shape[0]
    rows = weights[0].shape[1]
    group = 1
    while rows * group < 384 and weights[0].shape[0] % (2 * group) == 0:
        group *= 2
    counts = [held.shape[0] // group for held in weights[::2]]
    starts = [sum(counts[:i]) for i in range(len(counts))]
    specs = []
    for start, count in zip(starts, counts):
        spec = pl.BlockSpec(
            (group, rows, width_all),
            lambda h, me, start=start, count=count: (jnp.clip(h - start, 0, count - 1), 0, 0),
        )
        specs += [spec, spec]
    shape = by_cell.shape[1:]
    whole = pl.BlockSpec(shape, lambda h, me: (0, 0, 0))
    cells = pl.BlockSpec(by_cell.shape, lambda h, me: (0, 0, 0, 0))
    return pl.pallas_call(
        functools.partial(mlp_kernel, packing, sources, counts),
        grid_spec=pltpu.PrefetchScalarGridSpec(
            num_scalar_prefetch=1,
            grid=(sum(counts),),
            in_specs=[cells, pl.BlockSpec((width_all, 1), lambda h, me: (0, 0)), *specs],
            out_specs=[whole] * sources,
            scratch_shapes=[
                pltpu.VMEM((width_all, packing.wide), jnp.float32),
                pltpu.VMEM((width_all, packing.wide), jnp.bfloat16),
                pltpu.VMEM((width_all, packing.wide), jnp.float32),
            ],
        ),
        out_shape=[jax.ShapeDtypeStruct(shape, jnp.bfloat16)] * sources,
        compiler_params=PARAMS,
        cost_estimate=microseconds(1),
        name="mlp",
    )(me, by_cell, gain, *weights)


def add_kernel(packing, sources, me_ref, *refs):
    piece_refs, field_ref = refs[:sources], refs[sources]
    out_ref, cells_ref, update_ref = refs[-3:]
    me = me_ref[0]
    rows = update_ref.shape[0] // sources
    width = field_ref.shape[2]
    for shift in range(sources):
        sender = lax.rem(me + sources - shift, sources)

        def put(i, piece):
            cells_ref[:, i * LANES : (i + 1) * LANES] = piece

        packing.load(piece_refs[shift], 0, put)
        for row in range(rows):
            update_ref[sender * rows + row] = cells_ref[:, row * width : (row + 1) * width]
    update = jnp.transpose(update_ref[...], (1, 0, 2))
    out_ref[...] = (field_ref[...].astype(jnp.float32) + update).astype(out_ref.dtype)


def add_rows(packing, me, pieces, field, done, place, row_count):
    sources = len(pieces)
    width = field.shape[2]
    block = packing.block
    rows_of = pl.BlockSpec((block, row_count, width), lambda c, me: (c, place, 0))
    specs = [pl.BlockSpec((1, packing.rows, LANES), lambda c, me: (c, 0, 0))] * sources + [rows_of]
    operands = [me, *pieces, field]
    if done is not None:
        specs.append(pl.BlockSpec(memory_space=pl.ANY))
        operands.append(done)
    return pl.pallas_call(
        functools.partial(add_kernel, packing, sources),
        grid_spec=pltpu.PrefetchScalarGridSpec(
            num_scalar_prefetch=1,
            grid=(packing.blocks,),
            in_specs=specs,
            out_specs=rows_of,
            scratch_shapes=[
                pltpu.VMEM((block, packing.wide), jnp.float32),
                pltpu.VMEM((row_count, block, width), jnp.float32),
            ],
        ),
        out_shape=jax.ShapeDtypeStruct(field.shape, jnp.bfloat16),
        input_output_aliases={len(operands) - 1: 0} if done is not None else {},
        compiler_params=PARAMS,
        cost_estimate=microseconds(4),
        name="add",
    )(*operands)


def shifted(array, axis, shift):
    count = lax.axis_size(axis)
    return lax.ppermute(array, axis, [(i, (i + shift) % count) for i in range(count)])


def exchanged(array, axis, bit):
    return lax.ppermute(array, axis, [(i, i ^ bit) for i in range(lax.axis_size(axis))])


def stack_kernel(counts, *refs):
    *in_refs, out_ref = refs
    step, first = pl.program_id(0), 0
    for ref, count in zip(in_refs, counts):

        @pl.when(jnp.logical_and(step >= first, step < first + count))
        def _(ref=ref):
            out_ref[...] = ref[...]

        first += count


def stacked(*arrays):
    counts = [array.shape[0] for array in arrays]
    block = (1, *arrays[0].shape[1:])
    specs = [
        pl.BlockSpec(block, lambda i, start=sum(counts[:k]), count=count: (jnp.clip(i - start, 0, count - 1), 0, 0))
        for k, count in enumerate(counts)
    ]
    return pl.pallas_call(
        functools.partial(stack_kernel, counts),
        grid=(sum(counts),),
        in_specs=specs,
        out_specs=pl.BlockSpec(block, lambda i: (i, 0, 0)),
        out_shape=jax.ShapeDtypeStruct((sum(counts), *block[1:]), arrays[0].dtype),
        compiler_params=PARAMS,
        cost_estimate=microseconds(1),
        name="stack",
    )(*arrays)


def after_all(arrays, *others):
    return lax.optimization_barrier((arrays, others))[0]


def on_device(weather, lon_taps, latitude_taps, norm_gain, up_weight, down_weight):
    chan_count, row_total, width = weather.shape
    sources, tiles = lax.axis_size("chan"), lax.axis_size("tile")
    me = lax.axis_index("chan").astype(jnp.int32)[None]
    with jax.named_scope("halo"):
        before = shifted(weather[:, :, width - BORDER :], "tile", 1)
        after = shifted(weather[:, :, :BORDER], "tile", tiles - 1)
    shard = jnp.concatenate([up_weight.T, down_weight.T], axis=0)[None]
    with jax.named_scope("wz"):
        far = [shard]
        bit = sources // 2
        while bit > 1:
            far = far + [exchanged(piece, "chan", bit) for piece in far]
            bit //= 2
        near = exchanged(shard, "chan", 1)
    bits = []
    bit = tiles // 2
    while bit > 1:
        bits.append(bit)
        bit //= 2
    with jax.named_scope("wx0"):
        across = exchanged(shard, "tile", bits[0])
    field = jnp.transpose(weather, (1, 0, 2))
    before = jnp.transpose(before, (1, 0, 2))
    after = jnp.transpose(after, (1, 0, 2))
    lon, lat = lon_taps.T, latitude_taps.T
    rows = row_total // CHUNKS
    packing = Packing(chan_count, rows // sources * width)

    def spread(place):
        spatial = convolve(packing, sources, field, before, after, lon, lat, place, rows)
        with jax.named_scope(f"in{place}"):
            return spatial, lax.all_to_all(spatial, "chan", split_axis=0, concat_axis=0, tiled=True)

    by_cell = []
    spatial, cells = spread(0)
    by_cell.append(cells)
    lon, far, near, across = after_all((lon, far, near, across), spatial)
    with jax.named_scope("wz1"):
        rest = [exchanged(piece, "chan", 1) for piece in far[1:]]
    spatial, cells = spread(1)
    by_cell.append(cells)
    lon, rest, across = after_all((lon, rest, across), spatial, by_cell[0])
    others = stacked(*far[1:], near, *rest)
    with jax.named_scope("wx1"):
        others_across = exchanged(others, "tile", bits[0])
    spatial, cells = spread(2)
    by_cell.append(cells)
    lon, others = after_all((lon, others), spatial, by_cell[1])
    held = stacked(shard, across, others)
    for bit in bits[1:]:
        held = stacked(held, exchanged(held, "tile", bit))
    with jax.named_scope("wc0"):
        received = exchanged(held, "tile", 1)
    spatial, cells = spread(3)
    by_cell.append(cells)
    others_across = after_all(others_across, spatial)
    for bit in bits[1:]:
        others_across = stacked(others_across, exchanged(others_across, "tile", bit))
    with jax.named_scope("wc1"):
        others_received = exchanged(others_across, "tile", 1)
    weights = [held, received, others_across, others_received]
    gain = norm_gain[:, None]
    me = after_all(me, by_cell[2])
    updates = []
    for chunk in range(CHUNKS):
        pieces = mlp(packing, me, by_cell[chunk], gain, weights)
        with jax.named_scope(f"out{chunk}"):
            updates.append([pieces[0]] + [shifted(pieces[s], "chan", s) for s in range(1, sources)])
        me = after_all(me, pieces[0], updates[chunk - 1][1:] if chunk else by_cell[CHUNKS - 1])
    mixed = None
    for chunk in range(CHUNKS):
        mixed = add_rows(packing, me, updates[chunk], weather, mixed, chunk, rows)
    return mixed


def solution(mesh):
    return jax.shard_map(
        on_device,
        mesh=mesh,
        in_specs=(
            P("chan", "parts", "tile"),
            P(None, "chan"),
            P(None, "chan"),
            P(),
            P(None, ("tile", "chan")),
            P(None, ("tile", "chan")),
        ),
        out_specs=P("chan", "parts", "tile"),
        check_vma=False,
    )
```

```python
import functools

import jax
import jax.numpy as jnp
from jax import lax
from jax.experimental import pallas as pl
from jax.experimental.pallas import tpu as pltpu
from jax.sharding import PartitionSpec as P

KERNEL_TAPS = 9
DILATION_STEP = 2
BORDER = DILATION_STEP * (KERNEL_TAPS // 2)
LANES = 128
SUBLANES = 8
CHUNKS = 4
PARAMS = pltpu.CompilerParams(vmem_limit_bytes=60 * 1024 * 1024)


def microseconds(count):
    return pl.CostEstimate(flops=int(count * 1.15e9), bytes_accessed=1024, transcendentals=0)


def round_up(value, step):
    return -(-value // step) * step


class Packing:
    def __init__(self, chan_count, cells):
        self.block = 64 if chan_count % 64 == 0 else 32
        self.blocks = chan_count // self.block
        unit = LANES * SUBLANES // self.block
        used = round_up(cells, unit)
        self.full = used // LANES
        self.groups = []
        row, offset, size = self.full * self.block, 0, LANES // 2
        while size >= unit:
            if used % LANES & size:
                self.groups.append((row, offset, size))
                row += self.block * size // LANES
                offset += size
            size //= 2
        self.rows = row
        self.wide = round_up(cells, LANES)

    def store(self, ref, lead, load):
        for i in range(self.full):
            ref[lead, i * self.block : (i + 1) * self.block, :] = load(i).astype(ref.dtype)
        if not self.groups:
            return
        tail = load(self.full)
        for row, offset, size in self.groups:
            count = self.block * size // LANES
            lane = lax.broadcasted_iota(jnp.int32, (count, LANES), 1)
            packed = None
            for g in range(LANES // size):
                piece = tail[g * count : (g + 1) * count]
                if (g * size - offset) % LANES:
                    piece = pltpu.roll(piece, (g * size - offset) % LANES, 1)
                packed = piece if packed is None else jnp.where(lane >= g * size, piece, packed)
            ref[lead, row : row + count, :] = packed.astype(ref.dtype)

    def load(self, ref, lead, store):
        for i in range(self.full):
            store(i, ref[lead, i * self.block : (i + 1) * self.block, :].astype(jnp.float32))
        if not self.groups:
            return
        lane = lax.broadcasted_iota(jnp.int32, (self.block, LANES), 1)
        tail = None
        for row, offset, size in self.groups:
            count = self.block * size // LANES
            packed = ref[lead, row : row + count, :].astype(jnp.float32)
            pieces = []
            for g in range(LANES // size):
                turn = (offset - g * size) % LANES
                pieces.append(pltpu.roll(packed, turn, 1) if turn else packed)
            whole = jnp.concatenate(pieces, axis=0)
            tail = whole if tail is None else jnp.where(lane >= offset, whole, tail)
        store(self.full, tail)


def conv_kernel(packing, sources, rows, first_row, low, me_ref, *refs):
    outs = 1 if refs[-3].shape[0] == sources else sources
    *field_refs, lon_ref, lat_ref = refs[: -outs - 2]
    out_refs, (base_ref, cells_ref) = refs[-outs - 2 : -2], refs[-2:]
    start = 0 if outs == 1 else sources - me_ref[0]
    width = field_refs[0].shape[2]
    held_rows, block, wide = base_ref.shape
    group = field_refs[0].shape[0]
    for held in range(held_rows):
        field_ref, before_ref, after_ref = field_refs[held // group * 3 : held // group * 3 + 3]
        row = held % group
        base_ref[held, :, 0:width] = field_ref[row].astype(jnp.float32)
        base_ref[held, :, width : width + BORDER] = after_ref[row].astype(jnp.float32)
        base_ref[held, :, wide - BORDER : wide] = before_ref[row].astype(jnp.float32)
    part = 16

    def some_channels(index, _):
        chans = pl.ds(pl.multiple_of(index * part, part), part)
        lon = [jnp.broadcast_to(lon_ref[chans, t : t + 1], (part, wide)) for t in range(KERNEL_TAPS)]
        lat = [jnp.broadcast_to(lat_ref[chans, t : t + 1], (part, wide)) for t in range(KERNEL_TAPS)]
        for out_row in range(sources * rows):
            total = None
            for t in range(KERNEL_TAPS):
                held = first_row + out_row + DILATION_STEP * (t - KERNEL_TAPS // 2) - low
                if 0 <= held < held_rows:
                    term = lat[t] * base_ref[held, chans, :]
                    total = term if total is None else total + term
            near = [total if turn == 0 else pltpu.roll(total, turn % wide, 1) for turn in (2, 0, -2)]
            result = None
            for a, turn in enumerate((6, 0, -6)):
                term = lon[3 * a] * near[0] + lon[3 * a + 1] * near[1] + lon[3 * a + 2] * near[2]
                term = pltpu.roll(term, turn % wide, 1) if turn else term
                result = term if result is None else result + term
            receiver, row = divmod(out_row, rows)
            slot = receiver if outs == 1 else lax.rem(receiver + start, sources)
            cells_ref[slot, chans, row * width : (row + 1) * width] = result[:, 0:width]
        return 0

    lax.fori_loop(0, block // part, some_channels, 0)
    for slot in range(sources):
        out_ref = out_refs[0].at[slot] if outs == 1 else out_refs[slot].at[0]
        packing.store(out_ref, 0, lambda i: cells_ref[slot, :, i * LANES : (i + 1) * LANES])


def convolve(packing, me, sources, outs, field, before, after, lon_taps, lat_taps, place, row_count):
    row_total, chan_count, width = field.shape
    block = packing.block
    wide = round_up(width + 2 * BORDER, LANES)
    reach = -(-BORDER // row_count)
    places = range(max(0, place - reach), min(row_total // row_count, place + 1 + reach))
    specs, operands = [], []
    for near in places:
        for array in (field, before, after):
            specs.append(pl.BlockSpec((row_count, block, array.shape[2]), lambda c, me, near=near: (near, c, 0)))
            operands.append(array)
    taps = pl.BlockSpec((block, KERNEL_TAPS), lambda c, me: (c, 0))
    count = sources // outs
    out = jax.ShapeDtypeStruct((count, packing.blocks, packing.rows, LANES), jnp.bfloat16)
    return pl.pallas_call(
        functools.partial(
            conv_kernel, packing, sources, row_count // sources, place * row_count, places[0] * row_count
        ),
        grid_spec=pltpu.PrefetchScalarGridSpec(
            num_scalar_prefetch=1,
            grid=(packing.blocks,),
            in_specs=[*specs, taps, taps],
            out_specs=[pl.BlockSpec((count, 1, packing.rows, LANES), lambda c, me: (0, c, 0, 0))] * outs,
            scratch_shapes=[
                pltpu.VMEM((len(places) * row_count, block, wide), jnp.float32),
                pltpu.VMEM((sources, block, packing.wide), jnp.float32),
            ],
        ),
        out_shape=[out] * outs,
        compiler_params=PARAMS,
        cost_estimate=microseconds(12),
        name="conv",
    )(me, *operands, lon_taps, lat_taps)


def mlp_kernel(packing, sources, arrays, counts, me_ref, *refs):
    x_refs, gain_ref = refs[:arrays], refs[arrays]
    weight_refs = refs[arrays + 1 : arrays + 1 + 2 * len(counts)]
    out_refs, (values, normed, total) = refs[-sources - 3 : -3], refs[-3:]
    step = pl.program_id(0)
    me = me_ref[0]
    block = packing.block
    chan_count = packing.blocks * block

    def channels(owner, lead):
        start = owner * chan_count + lead * block
        return pl.ds(start if isinstance(start, int) else pl.multiple_of(start, SUBLANES), block)

    @pl.when(step == 0)
    def _():
        for slot in range(sources):
            sender = slot if arrays == 1 else lax.rem(me + sources - slot, sources)
            x_ref = x_refs[0].at[slot] if arrays == 1 else x_refs[slot].at[0]
            for lead in range(packing.blocks):

                def put(i, piece, at=channels(sender, lead)):
                    values[at, i * LANES : (i + 1) * LANES] = piece

                packing.load(x_ref, lead, put)
        as_float = values[...]
        center = jnp.mean(as_float, axis=0, keepdims=True)
        deviation = as_float - center
        spread_sq = jnp.mean(deviation * deviation, axis=0, keepdims=True)
        normed[...] = (deviation * lax.rsqrt(spread_sq + 1e-06) * gain_ref[...]).astype(jnp.bfloat16)
        total[...] = jnp.zeros_like(total)

    first = 0
    for index, count in enumerate(counts):

        @pl.when(jnp.logical_and(step >= first, step < first + count))
        def _(pair=weight_refs[2 * index : 2 * index + 2]):
            hidden, down = [], []
            for ref in pair:
                whole = ref[...]
                half = whole.shape[1] // 2
                up_rows = whole[:, :half].reshape(-1, whole.shape[2])
                expanded = jnp.dot(up_rows, normed[...], preferred_element_type=jnp.float32)
                gelu = 0.5 * expanded * (1.0 + lax.erf(expanded * 0.7071067811865476))
                hidden.append(gelu.astype(jnp.bfloat16))
                down.append(whole[:, half:].reshape(-1, whole.shape[2]))
            total[...] += lax.dot_general(
                jnp.concatenate(down, axis=0),
                jnp.concatenate(hidden, axis=0),
                (((0,), (0,)), ((), ())),
                preferred_element_type=jnp.float32,
            )

        first += count

    @pl.when(step == pl.num_programs(0) - 1)
    def _():
        for shift in range(sources):
            owner = lax.rem(me + shift, sources)
            for lead in range(packing.blocks):
                at = channels(owner, lead)
                packing.store(out_refs[shift], lead, lambda i: total[at, i * LANES : (i + 1) * LANES])


def mlp(packing, me, by_cell, gain, weights):
    arrays = len(by_cell)
    sources = arrays * by_cell[0].shape[0]
    width_all = gain.shape[0]
    rows = weights[0].shape[1]
    group = 1
    while rows * group < 384 and weights[0].shape[0] % (2 * group) == 0:
        group *= 2
    counts = [held.shape[0] // group for held in weights[::2]]
    starts = [sum(counts[:i]) for i in range(len(counts))]
    specs = []
    for start, count in zip(starts, counts):
        spec = pl.BlockSpec(
            (group, rows, width_all),
            lambda h, me, start=start, count=count: (jnp.clip(h - start, 0, count - 1), 0, 0),
        )
        specs += [spec, spec]
    shape = by_cell[0].shape[1:]
    whole = pl.BlockSpec(shape, lambda h, me: (0, 0, 0))
    cells = pl.BlockSpec(by_cell[0].shape, lambda h, me: (0, 0, 0, 0))
    return pl.pallas_call(
        functools.partial(mlp_kernel, packing, sources, arrays, counts),
        grid_spec=pltpu.PrefetchScalarGridSpec(
            num_scalar_prefetch=1,
            grid=(sum(counts),),
            in_specs=[cells] * arrays + [pl.BlockSpec((width_all, 1), lambda h, me: (0, 0)), *specs],
            out_specs=[whole] * sources,
            scratch_shapes=[
                pltpu.VMEM((width_all, packing.wide), jnp.float32),
                pltpu.VMEM((width_all, packing.wide), jnp.bfloat16),
                pltpu.VMEM((width_all, packing.wide), jnp.float32),
            ],
        ),
        out_shape=[jax.ShapeDtypeStruct(shape, jnp.bfloat16)] * sources,
        compiler_params=PARAMS,
        cost_estimate=microseconds(13),
        name="mlp",
    )(me, *by_cell, gain, *weights)


def add_kernel(packing, sources, me_ref, *refs):
    piece_refs, field_ref = refs[:sources], refs[sources]
    out_ref, cells_ref, update_ref = refs[-3:]
    me = me_ref[0]
    rows = update_ref.shape[0] // sources
    width = field_ref.shape[2]
    for shift in range(sources):
        sender = lax.rem(me + sources - shift, sources)

        def put(i, piece):
            cells_ref[:, i * LANES : (i + 1) * LANES] = piece

        packing.load(piece_refs[shift], 0, put)
        for row in range(rows):
            update_ref[sender * rows + row] = cells_ref[:, row * width : (row + 1) * width]
    update = jnp.transpose(update_ref[...], (1, 0, 2))
    out_ref[...] = (field_ref[...].astype(jnp.float32) + update).astype(out_ref.dtype)


def add_rows(packing, me, pieces, field, done, place, row_count):
    sources = len(pieces)
    width = field.shape[2]
    block = packing.block
    rows_of = pl.BlockSpec((block, row_count, width), lambda c, me: (c, place, 0))
    specs = [pl.BlockSpec((1, packing.rows, LANES), lambda c, me: (c, 0, 0))] * sources + [rows_of]
    operands = [me, *pieces, field]
    if done is not None:
        specs.append(pl.BlockSpec(memory_space=pl.ANY))
        operands.append(done)
    return pl.pallas_call(
        functools.partial(add_kernel, packing, sources),
        grid_spec=pltpu.PrefetchScalarGridSpec(
            num_scalar_prefetch=1,
            grid=(packing.blocks,),
            in_specs=specs,
            out_specs=rows_of,
            scratch_shapes=[
                pltpu.VMEM((block, packing.wide), jnp.float32),
                pltpu.VMEM((row_count, block, width), jnp.float32),
            ],
        ),
        out_shape=jax.ShapeDtypeStruct(field.shape, jnp.bfloat16),
        input_output_aliases={len(operands) - 1: 0} if done is not None else {},
        compiler_params=PARAMS,
        cost_estimate=microseconds(4),
        name="add",
    )(*operands)


def shifted(array, axis, shift):
    count = lax.axis_size(axis)
    return lax.ppermute(array, axis, [(i, (i + shift) % count) for i in range(count)])


def exchanged(array, axis, bit):
    return lax.ppermute(array, axis, [(i, i ^ bit) for i in range(lax.axis_size(axis))])


def stack_kernel(counts, *refs):
    *in_refs, out_ref = refs
    step, first = pl.program_id(0), 0
    for ref, count in zip(in_refs, counts):

        @pl.when(jnp.logical_and(step >= first, step < first + count))
        def _(ref=ref):
            out_ref[...] = ref[...]

        first += count


def stacked(*arrays):
    counts = [array.shape[0] for array in arrays]
    block = (1, *arrays[0].shape[1:])
    specs = [
        pl.BlockSpec(block, lambda i, start=sum(counts[:k]), count=count: (jnp.clip(i - start, 0, count - 1), 0, 0))
        for k, count in enumerate(counts)
    ]
    return pl.pallas_call(
        functools.partial(stack_kernel, counts),
        grid=(sum(counts),),
        in_specs=specs,
        out_specs=pl.BlockSpec(block, lambda i: (i, 0, 0)),
        out_shape=jax.ShapeDtypeStruct((sum(counts), *block[1:]), arrays[0].dtype),
        compiler_params=PARAMS,
        cost_estimate=microseconds(13),
        name="stack",
    )(*arrays)


def after_all(arrays, *others):
    return lax.optimization_barrier((arrays, others))[0]


def on_device(weather, lon_taps, latitude_taps, norm_gain, up_weight, down_weight):
    chan_count, row_total, width = weather.shape
    sources, tiles = lax.axis_size("chan"), lax.axis_size("tile")
    me = lax.axis_index("chan").astype(jnp.int32)[None]
    with jax.named_scope("halo"):
        before = shifted(weather[:, :, width - BORDER :], "tile", 1)
        after = shifted(weather[:, :, :BORDER], "tile", tiles - 1)
    shard = jnp.concatenate([up_weight.T, down_weight.T], axis=0)[None]
    with jax.named_scope("wz"):
        far = [shard]
        bit = sources // 2
        while bit > 1:
            far = far + [exchanged(piece, "chan", bit) for piece in far]
            bit //= 2
        near = exchanged(shard, "chan", 1)
    bits = []
    bit = tiles // 2
    while bit > 1:
        bits.append(bit)
        bit //= 2
    with jax.named_scope("wx0"):
        across = exchanged(shard, "tile", bits[0])
    field = jnp.transpose(weather, (1, 0, 2))
    before = jnp.transpose(before, (1, 0, 2))
    after = jnp.transpose(after, (1, 0, 2))
    lon, lat = lon_taps.T, latitude_taps.T
    rows = row_total // CHUNKS
    packing = Packing(chan_count, rows // sources * width)

    def spread(place):
        outs = sources if place % 2 else 1
        spatial = convolve(packing, me, sources, outs, field, before, after, lon, lat, place, rows)
        with jax.named_scope(f"in{place}"):
            if outs == 1:
                return spatial, [lax.all_to_all(spatial[0], "chan", split_axis=0, concat_axis=0, tiled=True)]
            return spatial, [spatial[0]] + [shifted(spatial[s], "chan", s) for s in range(1, sources)]

    by_cell = []
    spatial, cells = spread(0)
    by_cell.append(cells)
    lon, far, near, across = after_all((lon, far, near, across), spatial[0])
    with jax.named_scope("wz1"):
        rest = [exchanged(piece, "chan", 1) for piece in far[1:]]
    spatial, cells = spread(1)
    by_cell.append(cells)
    lon = after_all(lon, spatial[0])
    rest, across = after_all((rest, across), spatial[0])
    others = stacked(*far[1:], near, *rest)
    with jax.named_scope("wx1"):
        others_across = exchanged(others, "tile", bits[0])
    spatial, cells = spread(2)
    by_cell.append(cells)
    held = stacked(shard, across, others)
    for bit in bits[1:]:
        held = stacked(held, exchanged(held, "tile", bit))
    lon, held = after_all((lon, held), spatial[0], by_cell[0], by_cell[1][1:])
    with jax.named_scope("wc0"):
        received = exchanged(held, "tile", 1)
    spatial, cells = spread(3)
    by_cell.append(cells)
    others_across = after_all(others_across, by_cell[2], by_cell[3][1])
    for bit in bits[1:]:
        others_across = stacked(others_across, exchanged(others_across, "tile", bit))
    with jax.named_scope("wc1"):
        others_received = exchanged(others_across, "tile", 1)
    weights = [held, received, others_across, others_received]
    gain = norm_gain[:, None]
    me = after_all(me, by_cell[2])
    updates = []
    for chunk in range(CHUNKS):
        pieces = mlp(packing, me, by_cell[chunk], gain, weights)
        with jax.named_scope(f"out{chunk}"):
            updates.append([pieces[0]] + [shifted(pieces[s], "chan", s) for s in range(1, sources)])
        me = after_all(me, pieces[0], updates[chunk - 1][1:] if chunk else by_cell[CHUNKS - 1][1:])
    mixed = None
    for chunk in range(CHUNKS):
        mixed = add_rows(packing, me, updates[chunk], weather, mixed, chunk, rows)
    return mixed


def solution(mesh):
    return jax.shard_map(
        on_device,
        mesh=mesh,
        in_specs=(
            P("chan", "parts", "tile"),
            P(None, "chan"),
            P(None, "chan"),
            P(),
            P(None, ("tile", "chan")),
            P(None, ("tile", "chan")),
        ),
        out_specs=P("chan", "parts", "tile"),
        check_vma=False,
    )
```

```python
import functools

import jax
import jax.numpy as jnp
from jax import lax
from jax.experimental import pallas as pl
from jax.experimental.pallas import tpu as pltpu
from jax.sharding import PartitionSpec as P

KERNEL_TAPS = 9
DILATION_STEP = 2
BORDER = DILATION_STEP * (KERNEL_TAPS // 2)
LANES = 128
SUBLANES = 8
CHUNKS = 4
PARAMS = pltpu.CompilerParams(vmem_limit_bytes=60 * 1024 * 1024)


def microseconds(count):
    return pl.CostEstimate(flops=int(count * 1.15e9), bytes_accessed=1024, transcendentals=0)


def round_up(value, step):
    return -(-value // step) * step


class Packing:
    def __init__(self, chan_count, cells):
        self.block = 64 if chan_count % 64 == 0 else 32
        self.blocks = chan_count // self.block
        unit = LANES * SUBLANES // self.block
        used = round_up(cells, unit)
        self.full = used // LANES
        self.groups = []
        row, offset, size = self.full * self.block, 0, LANES // 2
        while size >= unit:
            if used % LANES & size:
                self.groups.append((row, offset, size))
                row += self.block * size // LANES
                offset += size
            size //= 2
        self.rows = row
        self.wide = round_up(cells, LANES)

    def store(self, ref, lead, load):
        for i in range(self.full):
            ref[lead, i * self.block : (i + 1) * self.block, :] = load(i).astype(ref.dtype)
        if not self.groups:
            return
        tail = load(self.full)
        for row, offset, size in self.groups:
            count = self.block * size // LANES
            lane = lax.broadcasted_iota(jnp.int32, (count, LANES), 1)
            packed = None
            for g in range(LANES // size):
                piece = tail[g * count : (g + 1) * count]
                if (g * size - offset) % LANES:
                    piece = pltpu.roll(piece, (g * size - offset) % LANES, 1)
                packed = piece if packed is None else jnp.where(lane >= g * size, piece, packed)
            ref[lead, row : row + count, :] = packed.astype(ref.dtype)

    def load(self, ref, lead, store):
        for i in range(self.full):
            store(i, ref[lead, i * self.block : (i + 1) * self.block, :].astype(jnp.float32))
        if not self.groups:
            return
        lane = lax.broadcasted_iota(jnp.int32, (self.block, LANES), 1)
        tail = None
        for row, offset, size in self.groups:
            count = self.block * size // LANES
            packed = ref[lead, row : row + count, :].astype(jnp.float32)
            pieces = []
            for g in range(LANES // size):
                turn = (offset - g * size) % LANES
                pieces.append(pltpu.roll(packed, turn, 1) if turn else packed)
            whole = jnp.concatenate(pieces, axis=0)
            tail = whole if tail is None else jnp.where(lane >= offset, whole, tail)
        store(self.full, tail)


def conv_kernel(packing, sources, rows, first_row, low, me_ref, *refs):
    outs = 1 if refs[-3].shape[0] == sources else sources
    *field_refs, lon_ref, lat_ref = refs[: -outs - 2]
    out_refs, (base_ref, cells_ref) = refs[-outs - 2 : -2], refs[-2:]
    start = 0 if outs == 1 else sources - me_ref[0]
    width = field_refs[0].shape[2]
    held_rows, block, wide = base_ref.shape
    group = field_refs[0].shape[0]
    for held in range(held_rows):
        field_ref, before_ref, after_ref = field_refs[held // group * 3 : held // group * 3 + 3]
        row = held % group
        base_ref[held, :, 0:width] = field_ref[row].astype(jnp.float32)
        base_ref[held, :, width : width + BORDER] = after_ref[row].astype(jnp.float32)
        base_ref[held, :, wide - BORDER : wide] = before_ref[row].astype(jnp.float32)
    part = 16

    def some_channels(index, _):
        chans = pl.ds(pl.multiple_of(index * part, part), part)
        lon = [jnp.broadcast_to(lon_ref[chans, t : t + 1], (part, wide)) for t in range(KERNEL_TAPS)]
        lat = [jnp.broadcast_to(lat_ref[chans, t : t + 1], (part, wide)) for t in range(KERNEL_TAPS)]
        for out_row in range(sources * rows):
            total = None
            for t in range(KERNEL_TAPS):
                held = first_row + out_row + DILATION_STEP * (t - KERNEL_TAPS // 2) - low
                if 0 <= held < held_rows:
                    term = lat[t] * base_ref[held, chans, :]
                    total = term if total is None else total + term
            near = [total if turn == 0 else pltpu.roll(total, turn % wide, 1) for turn in (2, 0, -2)]
            result = None
            for a, turn in enumerate((6, 0, -6)):
                term = lon[3 * a] * near[0] + lon[3 * a + 1] * near[1] + lon[3 * a + 2] * near[2]
                term = pltpu.roll(term, turn % wide, 1) if turn else term
                result = term if result is None else result + term
            receiver, row = divmod(out_row, rows)
            slot = receiver if outs == 1 else lax.rem(receiver + start, sources)
            cells_ref[slot, chans, row * width : (row + 1) * width] = result[:, 0:width]
        return 0

    lax.fori_loop(0, block // part, some_channels, 0)
    for slot in range(sources):
        out_ref = out_refs[0].at[slot] if outs == 1 else out_refs[slot].at[0]
        packing.store(out_ref, 0, lambda i: cells_ref[slot, :, i * LANES : (i + 1) * LANES])


def convolve(packing, me, sources, outs, field, before, after, lon_taps, lat_taps, place, row_count):
    row_total, chan_count, width = field.shape
    block = packing.block
    wide = round_up(width + 2 * BORDER, LANES)
    reach = -(-BORDER // row_count)
    places = range(max(0, place - reach), min(row_total // row_count, place + 1 + reach))
    specs, operands = [], []
    for near in places:
        for array in (field, before, after):
            specs.append(pl.BlockSpec((row_count, block, array.shape[2]), lambda c, me, near=near: (near, c, 0)))
            operands.append(array)
    taps = pl.BlockSpec((block, KERNEL_TAPS), lambda c, me: (c, 0))
    count = sources // outs
    out = jax.ShapeDtypeStruct((count, packing.blocks, packing.rows, LANES), jnp.bfloat16)
    return pl.pallas_call(
        functools.partial(
            conv_kernel, packing, sources, row_count // sources, place * row_count, places[0] * row_count
        ),
        grid_spec=pltpu.PrefetchScalarGridSpec(
            num_scalar_prefetch=1,
            grid=(packing.blocks,),
            in_specs=[*specs, taps, taps],
            out_specs=[pl.BlockSpec((count, 1, packing.rows, LANES), lambda c, me: (0, c, 0, 0))] * outs,
            scratch_shapes=[
                pltpu.VMEM((len(places) * row_count, block, wide), jnp.float32),
                pltpu.VMEM((sources, block, packing.wide), jnp.float32),
            ],
        ),
        out_shape=[out] * outs,
        compiler_params=PARAMS,
        cost_estimate=microseconds(12),
        name="conv",
    )(me, *operands, lon_taps, lat_taps)


def mlp_kernel(packing, sources, arrays, counts, me_ref, *refs):
    x_refs, gain_ref = refs[:arrays], refs[arrays]
    weight_refs = refs[arrays + 1 : arrays + 1 + 2 * len(counts)]
    out_refs, (values, normed, total) = refs[-sources - 3 : -3], refs[-3:]
    step = pl.program_id(0)
    me = me_ref[0]
    block = packing.block
    chan_count = packing.blocks * block

    def channels(owner, lead):
        start = owner * chan_count + lead * block
        return pl.ds(start if isinstance(start, int) else pl.multiple_of(start, SUBLANES), block)

    @pl.when(step == 0)
    def _():
        for slot in range(sources):
            sender = slot if arrays == 1 else lax.rem(me + sources - slot, sources)
            x_ref = x_refs[0].at[slot] if arrays == 1 else x_refs[slot].at[0]
            for lead in range(packing.blocks):

                def put(i, piece, at=channels(sender, lead)):
                    values[at, i * LANES : (i + 1) * LANES] = piece

                packing.load(x_ref, lead, put)
        as_float = values[...]
        center = jnp.mean(as_float, axis=0, keepdims=True)
        deviation = as_float - center
        spread_sq = jnp.mean(deviation * deviation, axis=0, keepdims=True)
        normed[...] = (deviation * lax.rsqrt(spread_sq + 1e-06) * gain_ref[...]).astype(jnp.bfloat16)
        total[...] = jnp.zeros_like(total)

    first = 0
    for index, count in enumerate(counts):

        @pl.when(jnp.logical_and(step >= first, step < first + count))
        def _(pair=weight_refs[2 * index : 2 * index + 2]):
            hidden, down = [], []
            for ref in pair:
                whole = ref[...]
                half = whole.shape[1] // 2
                up_rows = whole[:, :half].reshape(-1, whole.shape[2])
                expanded = jnp.dot(up_rows, normed[...], preferred_element_type=jnp.float32)
                gelu = 0.5 * expanded * (1.0 + lax.erf(expanded * 0.7071067811865476))
                hidden.append(gelu.astype(jnp.bfloat16))
                down.append(whole[:, half:].reshape(-1, whole.shape[2]))
            total[...] += lax.dot_general(
                jnp.concatenate(down, axis=0),
                jnp.concatenate(hidden, axis=0),
                (((0,), (0,)), ((), ())),
                preferred_element_type=jnp.float32,
            )

        first += count

    @pl.when(step == pl.num_programs(0) - 1)
    def _():
        for shift in range(sources):
            owner = lax.rem(me + shift, sources)
            for lead in range(packing.blocks):
                at = channels(owner, lead)
                packing.store(out_refs[shift], lead, lambda i: total[at, i * LANES : (i + 1) * LANES])


def mlp(packing, me, by_cell, gain, weights):
    arrays = len(by_cell)
    sources = arrays * by_cell[0].shape[0]
    width_all = gain.shape[0]
    rows = weights[0].shape[1]
    group = 1
    while rows * group < 384 and weights[0].shape[0] % (2 * group) == 0:
        group *= 2
    counts = [held.shape[0] // group for held in weights[::2]]
    starts = [sum(counts[:i]) for i in range(len(counts))]
    specs = []
    for start, count in zip(starts, counts):
        spec = pl.BlockSpec(
            (group, rows, width_all),
            lambda h, me, start=start, count=count: (jnp.clip(h - start, 0, count - 1), 0, 0),
        )
        specs += [spec, spec]
    shape = by_cell[0].shape[1:]
    whole = pl.BlockSpec(shape, lambda h, me: (0, 0, 0))
    cells = pl.BlockSpec(by_cell[0].shape, lambda h, me: (0, 0, 0, 0))
    return pl.pallas_call(
        functools.partial(mlp_kernel, packing, sources, arrays, counts),
        grid_spec=pltpu.PrefetchScalarGridSpec(
            num_scalar_prefetch=1,
            grid=(sum(counts),),
            in_specs=[cells] * arrays + [pl.BlockSpec((width_all, 1), lambda h, me: (0, 0)), *specs],
            out_specs=[whole] * sources,
            scratch_shapes=[
                pltpu.VMEM((width_all, packing.wide), jnp.float32),
                pltpu.VMEM((width_all, packing.wide), jnp.bfloat16),
                pltpu.VMEM((width_all, packing.wide), jnp.float32),
            ],
        ),
        out_shape=[jax.ShapeDtypeStruct(shape, jnp.bfloat16)] * sources,
        compiler_params=PARAMS,
        cost_estimate=microseconds(13),
        name="mlp",
    )(me, *by_cell, gain, *weights)


def add_kernel(packing, sources, me_ref, *refs):
    piece_refs, field_ref = refs[:sources], refs[sources]
    out_ref, cells_ref, update_ref = refs[-3:]
    me = me_ref[0]
    rows = update_ref.shape[0] // sources
    width = field_ref.shape[2]
    for shift in range(sources):
        sender = lax.rem(me + sources - shift, sources)

        def put(i, piece):
            cells_ref[:, i * LANES : (i + 1) * LANES] = piece

        packing.load(piece_refs[shift], 0, put)
        for row in range(rows):
            update_ref[sender * rows + row] = cells_ref[:, row * width : (row + 1) * width]
    update = jnp.transpose(update_ref[...], (1, 0, 2))
    out_ref[...] = (field_ref[...].astype(jnp.float32) + update).astype(out_ref.dtype)


def add_rows(packing, me, pieces, field, done, place, row_count):
    sources = len(pieces)
    width = field.shape[2]
    block = packing.block
    rows_of = pl.BlockSpec((block, row_count, width), lambda c, me: (c, place, 0))
    specs = [pl.BlockSpec((1, packing.rows, LANES), lambda c, me: (c, 0, 0))] * sources + [rows_of]
    operands = [me, *pieces, field]
    if done is not None:
        specs.append(pl.BlockSpec(memory_space=pl.ANY))
        operands.append(done)
    return pl.pallas_call(
        functools.partial(add_kernel, packing, sources),
        grid_spec=pltpu.PrefetchScalarGridSpec(
            num_scalar_prefetch=1,
            grid=(packing.blocks,),
            in_specs=specs,
            out_specs=rows_of,
            scratch_shapes=[
                pltpu.VMEM((block, packing.wide), jnp.float32),
                pltpu.VMEM((row_count, block, width), jnp.float32),
            ],
        ),
        out_shape=jax.ShapeDtypeStruct(field.shape, jnp.bfloat16),
        input_output_aliases={len(operands) - 1: 0} if done is not None else {},
        compiler_params=PARAMS,
        cost_estimate=microseconds(4),
        name="add",
    )(*operands)


def shifted(array, axis, shift):
    count = lax.axis_size(axis)
    return lax.ppermute(array, axis, [(i, (i + shift) % count) for i in range(count)])


def exchanged(array, axis, bit):
    return lax.ppermute(array, axis, [(i, i ^ bit) for i in range(lax.axis_size(axis))])


def stack_kernel(counts, *refs):
    *in_refs, out_ref = refs
    step, first = pl.program_id(0), 0
    for ref, count in zip(in_refs, counts):

        @pl.when(jnp.logical_and(step >= first, step < first + count))
        def _(ref=ref):
            out_ref[...] = ref[...]

        first += count


def stacked(*arrays):
    counts = [array.shape[0] for array in arrays]
    block = (1, *arrays[0].shape[1:])
    specs = [
        pl.BlockSpec(block, lambda i, start=sum(counts[:k]), count=count: (jnp.clip(i - start, 0, count - 1), 0, 0))
        for k, count in enumerate(counts)
    ]
    return pl.pallas_call(
        functools.partial(stack_kernel, counts),
        grid=(sum(counts),),
        in_specs=specs,
        out_specs=pl.BlockSpec(block, lambda i: (i, 0, 0)),
        out_shape=jax.ShapeDtypeStruct((sum(counts), *block[1:]), arrays[0].dtype),
        compiler_params=PARAMS,
        cost_estimate=microseconds(13),
        name="stack",
    )(*arrays)


def after_all(arrays, *others):
    return lax.optimization_barrier((arrays, others))[0]


def on_device(weather, lon_taps, latitude_taps, norm_gain, up_weight, down_weight):
    chan_count, row_total, width = weather.shape
    sources, tiles = lax.axis_size("chan"), lax.axis_size("tile")
    me = lax.axis_index("chan").astype(jnp.int32)[None]
    with jax.named_scope("halo"):
        before = shifted(weather[:, :, width - BORDER :], "tile", 1)
        after = shifted(weather[:, :, :BORDER], "tile", tiles - 1)
    shard = jnp.concatenate([up_weight.T, down_weight.T], axis=0)[None]
    with jax.named_scope("wz"):
        far = [shard]
        bit = sources // 2
        while bit > 1:
            far = far + [exchanged(piece, "chan", bit) for piece in far]
            bit //= 2
        near = exchanged(shard, "chan", 1)
    bits = []
    bit = tiles // 2
    while bit > 1:
        bits.append(bit)
        bit //= 2
    field = jnp.transpose(weather, (1, 0, 2))
    before = jnp.transpose(before, (1, 0, 2))
    after = jnp.transpose(after, (1, 0, 2))
    lon, lat = lon_taps.T, latitude_taps.T
    rows = row_total // CHUNKS
    packing = Packing(chan_count, rows // sources * width)

    def spread(place):
        outs = sources if place % 2 else 1
        spatial = convolve(packing, me, sources, outs, field, before, after, lon, lat, place, rows)
        with jax.named_scope(f"in{place}"):
            if outs == 1:
                return spatial, [lax.all_to_all(spatial[0], "chan", split_axis=0, concat_axis=0, tiled=True)]
            return spatial, [spatial[0]] + [shifted(spatial[s], "chan", s) for s in range(1, sources)]

    by_cell = []
    spatial, cells = spread(0)
    by_cell.append(cells)
    lon, far, near = after_all((lon, far, near), spatial[0])
    with jax.named_scope("wx0"):
        across = exchanged(after_all(shard, spatial[0]), "tile", bits[0])
    with jax.named_scope("wz1"):
        rest = [exchanged(piece, "chan", 1) for piece in far[1:]]
    spatial, cells = spread(1)
    by_cell.append(cells)
    lon = after_all(lon, spatial[0])
    rest, across = after_all((rest, across), spatial[0])
    others = stacked(*far[1:], near, *rest)
    with jax.named_scope("wx1"):
        others_across = exchanged(others, "tile", bits[0])
    spatial, cells = spread(2)
    by_cell.append(cells)
    held = stacked(shard, across, others)
    for bit in bits[1:]:
        held = stacked(held, exchanged(held, "tile", bit))
    lon, held = after_all((lon, held), spatial[0], by_cell[0], by_cell[1][1:])
    with jax.named_scope("wc0"):
        received = exchanged(held, "tile", 1)
    spatial, cells = spread(3)
    by_cell.append(cells)
    others_across = after_all(others_across, by_cell[2], by_cell[3][1])
    for bit in bits[1:]:
        others_across = stacked(others_across, exchanged(others_across, "tile", bit))
    with jax.named_scope("wc1"):
        others_received = exchanged(others_across, "tile", 1)
    weights = [held, received, others_across, others_received]
    gain = norm_gain[:, None]
    me = after_all(me, by_cell[2])
    updates = []
    for chunk in range(CHUNKS):
        pieces = mlp(packing, me, by_cell[chunk], gain, weights)
        with jax.named_scope(f"out{chunk}"):
            updates.append([pieces[0]] + [shifted(pieces[s], "chan", s) for s in range(1, sources)])
        me = after_all(me, pieces[0], updates[chunk - 1][1:] if chunk else by_cell[CHUNKS - 1][1:])
    mixed = None
    for chunk in range(CHUNKS):
        mixed = add_rows(packing, me, updates[chunk], weather, mixed, chunk, rows)
    return mixed


def solution(mesh):
    return jax.shard_map(
        on_device,
        mesh=mesh,
        in_specs=(
            P("chan", "parts", "tile"),
            P(None, "chan"),
            P(None, "chan"),
            P(),
            P(None, ("tile", "chan")),
            P(None, ("tile", "chan")),
        ),
        out_specs=P("chan", "parts", "tile"),
        check_vma=False,
    )
```
